32 devices in a mesh: groups: 2 (over x), ctx: 16 (over z, y, core).
Axes of the slice: x: 2, y: 2, z: 4, core: 2. Of those that a mesh axis runs over, the one named last changes fastest.
Arguments:
- queries: bfloat16 [16384, 3584], P(('groups', 'ctx')), parts along dimension 0, may hold values from -48 to 48
- keys: bfloat16 [16384, 512], P(('groups', 'ctx')), parts along dimension 0, may hold values from -6 to 6
- values: bfloat16 [16384, 512], P(('groups', 'ctx')), parts along dimension 0, may hold values from -6 to 6
- out_grad: bfloat16 [16384, 3584], P(('groups', 'ctx')), parts along dimension 0, may hold values from -6 to 6
- links: int32 [128, 4], P(('groups', 'ctx')), parts along dimension 0, may hold values from -1 to 3, as said below
- header_blocks: int32 [8], P('groups'), parts along dimension 0, may hold values from 0 to 59, as said below
Outputs:
- query_grad: bfloat16 [16384, 3584], P(('groups', 'ctx')), parts along dimension 0
- key_gradient_array: float32 [16384, 512], P(('groups', 'ctx')), parts along dimension 0
- value_gradient_array: float32 [16384, 512], P(('groups', 'ctx')), parts along dimension 0
The draws below stay inside these ranges and needn't reach their ends.
There are 2 independent parts, one for each index of `groups`. The reference program is written for one: setup_inputs(seed, part) draws one part's arguments, and reference() takes and returns one part's arrays. A program takes and returns all parts, laid end to end along the dimension named above; each array names one. Nothing has to cross between parts.
Inputs may be any that keep to these rules, and one draw needn't show every extreme that they name: `header_blocks`: strictly increasing; no two header blocks lie among the same aligned 4 blocks, and none lies among the last 4 blocks. Non-empty entries of one row are distinct header numbers whose header block ends before the row's window part begins (header_blocks[links[b, l]] <= b - 256 / 128 - 1). The last row has no empty entry.
All inputs are finite; a program needn't handle non-finite values.
Results may differ from the reference program's by a relative error of at most 0.012.
Values may be sent and summed in bfloat16 or wider, within the bound.
A program may use at most 192 MiB of HBM per device.

```python
import jax
import jax.numpy as jnp
from jax import lax

QUERY_HEADS = 28
KEY_VALUE_HEADS = 4
HEAD_SIZE = 128
BLK = 128
WIN = 256
LINKS = 4
BLK_DEV = 4
SEQUENCE_SPAN = 8192
NQB = 64
NH = 4


def query_key_pair(key):
    query_key = jax.random.fold_in(key, 11)
    key_lookup_name = jax.random.fold_in(key, 12)
    query_out = jnp.clip(jax.random.normal(query_key, (SEQUENCE_SPAN, QUERY_HEADS * HEAD_SIZE), jnp.float32), -6.0, 6.0)
    key_result_output = jnp.clip(jax.random.normal(key_lookup_name, (SEQUENCE_SPAN, KEY_VALUE_HEADS * HEAD_SIZE), jnp.float32), -6.0, 6.0)
    return (query_out, key_result_output)


def draw_queries(key, part):
    return query_key_pair(key)[0].astype(jnp.bfloat16)


def draw_keys(key, part):
    return query_key_pair(key)[1].astype(jnp.bfloat16)


def header_layout(key):
    base = jax.random.fold_in(key, 21)
    device_count = NQB // BLK_DEV
    middle = jax.random.permutation(jax.random.fold_in(base, 1), device_count - 3)[:NH - 2].astype(jnp.int32) + 1
    owners = jnp.sort(jnp.concatenate([jnp.zeros((1,), jnp.int32), middle, jnp.full((1,), device_count - 2, jnp.int32)]))
    offsets = jax.random.randint(jax.random.fold_in(base, 2), (NH,), 0, BLK_DEV).astype(jnp.int32)
    offsets = offsets.at[0].set(0).at[NH - 1].set(BLK_DEV - 1)
    return (owners * BLK_DEV + offsets).astype(jnp.int32)


def draw_header_blocks(key, part):
    return header_layout(key)


def draw_links(key, part):
    blocks = header_layout(key)
    base = jax.random.fold_in(key, 31)
    row_ids = jnp.arange(NQB, dtype=jnp.int32)
    slot_ids = jnp.arange(NH, dtype=jnp.int32)
    eligible = blocks[None, :] <= row_ids[:, None] - WIN // BLK - 1
    noise = jax.random.randint(jax.random.fold_in(base, 1), (NQB, NH), 0, 1 << 16).astype(jnp.int32)
    score = noise * NH + slot_ids[None, :]
    forced = (row_ids[:, None] == NQB - 1) & (slot_ids[None, :] == NH - 1)
    score = score + eligible.astype(jnp.int32) * (1 << 25) + forced.astype(jnp.int32) * (1 << 24)
    ignored, chosen = lax.top_k(score, LINKS)
    density = jax.random.randint(jax.random.fold_in(base, 2), (NQB // BLK_DEV,), 0, LINKS + 1).astype(jnp.int32)
    row_cap = jnp.repeat(density, BLK_DEV)
    counts = jax.random.randint(jax.random.fold_in(base, 3), (NQB,), 0, row_cap + 1).astype(jnp.int32)
    counts = jnp.where(row_ids == NQB - 1, LINKS, counts)
    usable = jnp.take_along_axis(eligible, chosen, axis=1)
    keep_entry = (jnp.arange(LINKS, dtype=jnp.int32)[None, :] < counts[:, None]) & usable
    return jnp.where(keep_entry, chosen, -1).astype(jnp.int32)


def levels(own_key, dims, split, low, high):
    factor_of, own = 1.0, jax.random.fold_in(own_key, 6)
    for axis_at, parts in split:
        draws = jnp.exp(jax.random.uniform(jax.random.fold_in(own, axis_at), (parts,), jnp.float32, low / len(split), high / len(split)))
        factor_of = factor_of * jnp.repeat(draws, dims[axis_at] // parts).reshape([-1 if axis == axis_at else 1 for axis in range(len(dims))])
    return factor_of


def centred(rng, extent, scale, limit, cuts=(), kind=jnp.bfloat16):
    values = scale * jax.random.normal(rng, extent, jnp.float32)
    if cuts:
        values = values * levels(rng, extent, cuts, -0.22, 0.18)
    return jnp.clip(values, -limit, limit).astype(kind)


def setup_inputs(seed: int = 0, part: int = 0) -> dict:
    key_list = jax.random.split(jax.random.key(seed), 7)
    part_splits = jax.random.split(jax.random.fold_in(key_list[6], part), 7)
    return {
        "queries": draw_queries(jax.random.fold_in(jax.random.fold_in(key_list[6], part), 71), part),
        "keys": draw_keys(jax.random.fold_in(jax.random.fold_in(key_list[6], part), 71), part),
        "values": centred(part_splits[2], (SEQUENCE_SPAN, KEY_VALUE_HEADS * HEAD_SIZE), 1.0, 6.0, ((0, 16),)),
        "out_grad": centred(part_splits[3], (SEQUENCE_SPAN, QUERY_HEADS * HEAD_SIZE), 1.0, 6.0, ((0, 16),)),
        "links": draw_links(jax.random.fold_in(jax.random.fold_in(key_list[6], part), 71), part),
        "header_blocks": draw_header_blocks(jax.random.fold_in(jax.random.fold_in(key_list[6], part), 71), part),
    }


def block_grads(query_row_block, gradient_row_block, key_row_block, value_row_block, is_valid):
    row_total_count = query_row_block.shape[0]
    key_total_count = key_row_block.shape[0]
    queries_each_group = QUERY_HEADS // KEY_VALUE_HEADS
    factor = float(HEAD_SIZE) ** -0.5
    highest = lax.Precision.HIGHEST
    query_four_axes = query_row_block.astype(jnp.float32).reshape(row_total_count, KEY_VALUE_HEADS, queries_each_group, HEAD_SIZE)
    gradient_four_axes = gradient_row_block.astype(jnp.float32).reshape(row_total_count, KEY_VALUE_HEADS, queries_each_group, HEAD_SIZE)
    key_three_axes = key_row_block.astype(jnp.float32).reshape(key_total_count, KEY_VALUE_HEADS, HEAD_SIZE)
    value_three_axes = value_row_block.astype(jnp.float32).reshape(key_total_count, KEY_VALUE_HEADS, HEAD_SIZE)
    scores = jnp.einsum("qgrd,kgd->gqrk", query_four_axes, key_three_axes, precision=highest) * factor
    scores = jnp.where(is_valid[None, :, None, :], scores, -1e30)
    row_max = jnp.max(scores, axis=-1, keepdims=True)
    weights = jnp.exp(scores - row_max)
    attend = weights / jnp.sum(weights, axis=-1, keepdims=True)
    d_attend = jnp.einsum("qgrd,kgd->gqrk", gradient_four_axes, value_three_axes, precision=highest)
    row_delta = jnp.sum(attend * d_attend, axis=-1, keepdims=True)
    d_scores = (attend * (d_attend - row_delta) * factor).astype(jnp.bfloat16).astype(jnp.float32)
    attend_low = attend.astype(jnp.bfloat16).astype(jnp.float32)
    query_grad = jnp.einsum("gqrk,kgd->qgrd", d_scores, key_three_axes, precision=highest)
    key_gradient_array = jnp.einsum("gqrk,qgrd->kgd", d_scores, query_four_axes, precision=highest)
    value_gradient_array = jnp.einsum("gqrk,qgrd->kgd", attend_low, gradient_four_axes, precision=highest)
    key_value_gradient = jnp.concatenate([key_gradient_array.reshape(key_total_count, KEY_VALUE_HEADS * HEAD_SIZE), value_gradient_array.reshape(key_total_count, KEY_VALUE_HEADS * HEAD_SIZE)], axis=1)
    return query_grad.reshape(row_total_count, QUERY_HEADS * HEAD_SIZE), key_value_gradient


def reference(queries, keys, values, out_grad, links, header_blocks):
    seq_len = queries.shape[0]
    block_total = seq_len // BLK
    half_width = keys.shape[1]
    kv_full = jnp.concatenate([keys, values], axis=1)
    kv_width = kv_full.shape[1]
    padded = jnp.concatenate([jnp.zeros((WIN, kv_width), kv_full.dtype), kv_full], axis=0)
    window_span = WIN + BLK

    def one_block(acc, block_id):
        row_start = (block_id * BLK).astype(jnp.int32)
        query_row_block = lax.dynamic_slice_in_dim(queries, row_start, BLK, 0)
        gradient_row_block = lax.dynamic_slice_in_dim(out_grad, row_start, BLK, 0)
        window = lax.dynamic_slice_in_dim(padded, row_start, window_span, 0)
        entries = links[block_id]
        is_live = entries >= 0
        safe_slot = jnp.where(is_live, entries, 0).astype(jnp.int32)
        header_ids = header_blocks[safe_slot].astype(jnp.int32)
        pieces = [lax.dynamic_slice_in_dim(kv_full, (header_ids[slot] * BLK).astype(jnp.int32), BLK, 0) for slot in range(LINKS)]
        key_tile = jnp.concatenate([window] + pieces, axis=0)
        q_pos = row_start + jnp.arange(BLK, dtype=jnp.int32)
        k_pos = row_start - WIN + jnp.arange(window_span, dtype=jnp.int32)
        near_ok = (k_pos[None, :] <= q_pos[:, None]) & (q_pos[:, None] - k_pos[None, :] < WIN) & (k_pos[None, :] >= 0)
        far_ok = jnp.broadcast_to(jnp.repeat(is_live, BLK)[None, :], (BLK, LINKS * BLK))
        is_valid = jnp.concatenate([near_ok, far_ok], axis=1)
        query_grad, key_value_gradient = block_grads(query_row_block, gradient_row_block, key_tile[:, :half_width], key_tile[:, half_width:], is_valid)
        current = lax.dynamic_slice_in_dim(acc, row_start, window_span, 0)
        acc = lax.dynamic_update_slice_in_dim(acc, current + key_value_gradient[:window_span], row_start, 0)
        for slot in range(LINKS):
            target = (WIN + header_ids[slot] * BLK).astype(jnp.int32)
            extra = key_value_gradient[window_span + slot * BLK: window_span + (slot + 1) * BLK] * is_live[slot].astype(jnp.float32)
            current = lax.dynamic_slice_in_dim(acc, target, BLK, 0)
            acc = lax.dynamic_update_slice_in_dim(acc, current + extra, target, 0)
        return acc, query_grad.astype(jnp.bfloat16)

    start_acc = jnp.zeros((seq_len + WIN, kv_width), jnp.float32)
    acc, dq_blocks = lax.scan(one_block, start_acc, jnp.arange(block_total, dtype=jnp.int32))
    query_out = dq_blocks.reshape(seq_len, QUERY_HEADS * HEAD_SIZE)
    full_grad = acc[WIN:]
    return query_out, full_grad[:, :half_width], full_grad[:, half_width:]
```

```python
import functools
import math

import jax
import jax.numpy as jnp
from jax import lax
from jax.experimental import pallas as pl
from jax.experimental.pallas import tpu as pltpu
from jax.sharding import PartitionSpec as P

QUERY_HEADS = 28
KVH = 4
HEAD_SIZE = 128
BLK = 128
WIN = 256
LINKS = 4
REP = QUERY_HEADS // KVH
WIDE = REP * HEAD_SIZE
FACTOR = float(HEAD_SIZE) ** (-0.5)
EXP2_FACTOR = FACTOR * math.log2(math.e)
NT = (((1,), (1,)), ((), ()))
MESH = pl.DeviceIdType.MESH
F32 = jnp.float32
BF16 = jnp.bfloat16


def dot(a, b, dims=(((1,), (0,)), ((), ()))):
    return lax.dot_general(a, b, dims, preferred_element_type=F32)


def log2(n):
    return n.bit_length() - 1


def kernel(n, nh, bc, links, headers, q_ref, o_ref, k_ref, v_ref, dq_ref, kg_ref, vg_ref,
           kvx, raw, tabs, rtabs, kcat, vcat, ds_s, p_s, near, back_s, back_r, far, s0, r0, s1, r1, red, p2, r2,
           win_sem, gat_send, gat_recv, back_sem, rs_sem, r1_sem, r2_sem):
    g = pl.program_id(0)
    b = pl.program_id(1)
    me = lax.axis_index("ctx")
    core = lax.rem(me, 2)
    pair = me // 2
    k = log2(n)
    raw_steps = log2(raw.shape[1])
    tab_steps = k - raw_steps
    rp = BLK // n
    rows = bc * BLK

    def to(d):
        return {"ctx": d}

    holders = [headers[h] // bc for h in range(nh)]

    def exchange(c, s):
        partner = jnp.bitwise_xor(me, 1 << (k - 1 - s))
        if s < raw_steps:
            src, dst = raw.at[c, pl.ds(0, 1 << s)], raw.at[c, pl.ds(1 << s, 1 << s)]
        else:
            src, dst = tabs.at[s - raw_steps, c], rtabs.at[s - raw_steps, c]
        return pltpu.make_async_remote_copy(src_ref=src, dst_ref=dst, send_sem=gat_send.at[c, s],
                                            recv_sem=gat_recv.at[c, s], device_id=to(partner), device_id_type=MESH)

    def apart(i):
        return sum(((i >> s) & 1) << (k - 1 - s) for s in range(raw_steps))

    def gather_event(c, j):
        if j > 0:
            exchange(c, j - 1).wait_recv()
        if j == raw_steps:
            for h in range(nh):
                x = jnp.bitwise_xor(me, holders[h])
                flags = [jnp.where(x == apart(i), 1.0, 0.0).astype(F32) for i in range(raw.shape[1])]
                for t in range(2):
                    tabs[0, c, t, h * BLK:(h + 1) * BLK] = sum(
                        raw[c, i, t].astype(F32) * f for i, f in enumerate(flags)).astype(BF16)
        elif j > raw_steps:
            s = j - raw_steps
            tabs[s, c] = (tabs[s - 1, c].astype(F32) + rtabs[s - 1, c].astype(F32)).astype(BF16)
        if j < k:
            exchange(c, j).start()

    def window(c):
        return pltpu.make_async_remote_copy(
            src_ref=kvx.at[c, :, pl.ds(rows, WIN)], dst_ref=kvx.at[c, :, pl.ds(0, WIN)], send_sem=win_sem.at[c, 0],
            recv_sem=win_sem.at[c, 1], device_id=to(lax.rem(me + 1, n)), device_id_type=MESH)

    def back(c):
        return pltpu.make_async_remote_copy(
            src_ref=back_s.at[c], dst_ref=back_r.at[c], send_sem=back_sem.at[c, 0],
            recv_sem=back_sem.at[c, 1], device_id=to(lax.rem(me + n - 1, n)), device_id_type=MESH)

    def core_copy(c):
        return pltpu.make_async_remote_copy(
            src_ref=s0.at[c, 1 - core], dst_ref=r0.at[c], send_sem=rs_sem.at[c, 0], recv_sem=rs_sem.at[c, 1],
            device_id=to(jnp.bitwise_xor(me, 1)), device_id_type=MESH)

    def scatter_copy(c, i):
        return pltpu.make_async_remote_copy(
            src_ref=s1.at[c, jnp.bitwise_xor(pair, i)], dst_ref=r1.at[c, i - 1], send_sem=r1_sem.at[c, 0],
            recv_sem=r1_sem.at[c, 1], device_id=to(jnp.bitwise_xor(me, 2 * i)), device_id_type=MESH)

    def return_copy(c, i):
        return pltpu.make_async_remote_copy(
            src_ref=p2.at[c, i - 1], dst_ref=r2.at[c, me], send_sem=r2_sem.at[c, 0],
            recv_sem=r2_sem.at[c, 1], device_id=to(jnp.bitwise_xor(me, i)), device_id_type=MESH)

    def rows_for(c, d):
        return sum(red[c, h] * jnp.where(holders[h] == d, 1.0, 0.0).astype(F32) for h in range(nh))

    def reduce_event(c, j):
        if j == 0:
            for p in range(n):
                parts = [far[t, h * BLK + p * rp:h * BLK + (p + 1) * rp] for t in range(2) for h in range(nh)]
                s0[c, p % 2, p // 2] = jnp.concatenate(parts, axis=0).astype(BF16)
            core_copy(c).start()
        if j == 1:
            core_copy(c).wait_recv()
            s1[c] = (s0[c, core].astype(F32) + r0[c].astype(F32)).astype(BF16)
            for i in range(1, n // 2):
                scatter_copy(c, i).start()
        if j == 2:
            pltpu.make_async_copy(r1.at[c], r1.at[c], r1_sem.at[c, 1]).wait()
            total = s1[c, pair].astype(F32)
            for i in range(n // 2 - 1):
                total = total + r1[c, i].astype(F32)
            for t in range(2):
                for h in range(nh):
                    at = (t * nh + h) * rp
                    red[c, h, t] = total[at:at + rp]
            for i in range(1, n):
                p2[c, i - 1] = rows_for(c, jnp.bitwise_xor(me, i))
                return_copy(c, i).start()
            r2[c, me] = rows_for(c, me)
        if j == 3:
            sent = p2.at[c]
            pltpu.make_async_copy(sent, sent, r2_sem.at[c, 1]).wait()
            flags = []
            for i in range(bc):
                flag = jnp.float32(0.0)
                for h in range(nh):
                    flag = jnp.where(headers[h] == me * bc + i, 1.0, flag)
                flags.append(flag)
            cols = pl.ds(pl.multiple_of(c * HEAD_SIZE, HEAD_SIZE), HEAD_SIZE)
            for t, out in ((0, kg_ref), (1, vg_ref)):
                own = jnp.concatenate([r2[c, p, t] for p in range(n)], axis=0)
                for i in range(bc):
                    out[i * BLK:(i + 1) * BLK, cols] = near[c, t, WIN + i * BLK:WIN + (i + 1) * BLK] + own * flags[i]

            @pl.when(me < n - 1)
            def _():
                back(c).wait_recv()
                for t, out in ((0, kg_ref), (1, vg_ref)):
                    out[rows - WIN:rows, cols] = out[rows - WIN:rows, cols] + back_r[c, t].astype(F32)

    @pl.when((g == 0) & (b == 0))
    def _():
        barrier = pltpu.get_barrier_semaphore()
        for i in range(1, n):
            pl.semaphore_signal(barrier, inc=1, device_id=to(jnp.bitwise_xor(me, i)), device_id_type=MESH)
        flags = []
        for i in range(bc):
            flag = jnp.float32(0.0)
            for h in range(nh):
                flag = jnp.where(headers[h] == me * bc + i, 1.0, flag)
            flags.append(flag)
        for c in range(KVH):
            cols = slice(c * HEAD_SIZE, (c + 1) * HEAD_SIZE)
            for t, ref in enumerate((k_ref, v_ref)):
                raw[c, 0, t] = sum(ref[i * BLK:(i + 1) * BLK, cols].astype(F32) * f for i, f in enumerate(flags)).astype(BF16)
            kvx[c, 0, WIN:] = k_ref[:, cols]
            kvx[c, 1, WIN:] = v_ref[:, cols]

        @pl.when(me == 0)
        def _():
            kvx[:, :, 0:WIN] = jnp.zeros((KVH, 2, WIN, HEAD_SIZE), BF16)

        pl.semaphore_wait(barrier, n - 1)
        gather_event(0, 0)

        @pl.when(me < n - 1)
        def _():
            for c in range(KVH):
                window(c).start()

        for j in range(1, k + 1):
            gather_event(0, j)
            if j <= 2:
                gather_event(1, j - 1)

    for j in range(1, k):
        step = bc - 1 if j == k - 1 else min(j - 1, bc - 1)
        first = 2 if j == 1 else 1

        @pl.when((b == step) & (g < KVH - 1) & (g + 1 >= first))
        def _():
            gather_event(g + 1, j)

    for j, step in ((1, min(1, bc - 1)), (2, min(2, bc - 1))):
        @pl.when((b == step) & (g > 0))
        def _():
            reduce_event(g - 1, j)

    @pl.when((b == 0) & (me > 0))
    def _():
        window(g).wait_recv()

    @pl.when(b == 0)
    def _():
        near[g] = jnp.zeros(near.shape[1:], F32)
        far[...] = jnp.zeros_like(far)

    first = me * bc + b
    row = pl.multiple_of(b * BLK, BLK)
    span = 3 * BLK
    kcat[0:span] = kvx[g, 0, pl.ds(row, span)]
    vcat[0:span] = kvx[g, 1, pl.ds(row, span)]
    kcat[span:] = tabs[tab_steps, g, 0]
    vcat[span:] = tabs[tab_steps, g, 1]

    dead0 = jnp.where(first >= 2, 0.0, 1e30).astype(F32)
    dead = [jnp.float32(0.0), jnp.where(first >= 1, 0.0, 1e30).astype(F32)]
    for h in range(nh):
        live = links[b, 0] == h
        for l in range(1, LINKS):
            live = live | (links[b, l] == h)
        dead.append(jnp.where(live, 0.0, 1e30).astype(F32))

    for a in range(0, REP, 2):
        heads = range(a, min(a + 2, REP))
        wide = len(heads) * BLK
        cols = slice(a * HEAD_SIZE, a * HEAD_SIZE + wide)
        key_at = lax.broadcasted_iota(jnp.int32, (BLK, wide), 0)
        query_at = lax.broadcasted_iota(jnp.int32, (BLK, wide), 1) & (BLK - 1)
        current = key_at <= query_at
        qs = jnp.concatenate([q_ref[:, h * HEAD_SIZE:(h + 1) * HEAD_SIZE] for h in heads], axis=0)
        os = jnp.concatenate([o_ref[:, h * HEAD_SIZE:(h + 1) * HEAD_SIZE] for h in heads], axis=0)
        st = dot(kcat[...], qs, NT)
        dpt = dot(vcat[...], os, NT)
        x = [jnp.where(current, st[2 * BLK:3 * BLK], st[0:BLK] - dead0)]
        d = [jnp.where(current, dpt[2 * BLK:3 * BLK], dpt[0:BLK])]
        for t in [1] + list(range(3, 3 + nh)):
            x.append(st[t * BLK:(t + 1) * BLK])
            d.append(dpt[t * BLK:(t + 1) * BLK])
        top = None
        for xt, dt in zip(x, dead):
            m = jnp.max(xt.reshape(BLK // 8, 8, wide), axis=0) - dt
            top = m if top is None else jnp.maximum(top, m)
        top = jnp.max(top, axis=0, keepdims=True)
        e = [jnp.exp2((xt - (top + dt)) * EXP2_FACTOR) for xt, dt in zip(x, dead)]
        norm = e[0]
        mixed = e[0] * d[0]
        for et, dt in zip(e[1:], d[1:]):
            norm = norm + et
            mixed = mixed + et * dt
        inverse = 1.0 / jnp.sum(norm, axis=0, keepdims=True)
        delta = jnp.sum(mixed, axis=0, keepdims=True) * inverse
        for t, (et, dt) in enumerate(zip(e, d)):
            p = et * inverse
            ds = p * (dt - delta)
            if t == 0:
                p_s[2 * BLK:3 * BLK, cols] = jnp.where(current, p, 0.0).astype(BF16)
                p_s[0:BLK, cols] = jnp.where(current, 0.0, p).astype(BF16)
                ds_s[2 * BLK:3 * BLK, cols] = jnp.where(current, ds, 0.0).astype(BF16)
                ds_s[0:BLK, cols] = jnp.where(current, 0.0, ds).astype(BF16)
            else:
                place = BLK if t == 1 else (t + 1) * BLK
                p_s[place:place + BLK, cols] = p.astype(BF16)
                ds_s[place:place + BLK, cols] = ds.astype(BF16)
    q_rows = jnp.concatenate([q_ref[:, h * HEAD_SIZE:(h + 1) * HEAD_SIZE] for h in range(REP)], axis=0)
    o_rows = jnp.concatenate([o_ref[:, h * HEAD_SIZE:(h + 1) * HEAD_SIZE] for h in range(REP)], axis=0)
    dk = dot(ds_s[...], q_rows) * FACTOR
    dv = dot(p_s[...], o_rows)
    far[0] += dk[span:]
    far[1] += dv[span:]
    near[g, 0, pl.ds(row, span)] += dk[0:span]
    near[g, 1, pl.ds(row, span)] += dv[0:span]

    @pl.when(b == bc - 1)
    def _():
        reduce_event(g, 0)

        @pl.when(me > 0)
        def _():
            back_s[g] = near[g, :, 0:WIN].astype(BF16)
            back(g).start()

    dqt = dot(kcat[...].T, ds_s[...]) * FACTOR
    for h in range(REP):
        cols = slice(h * HEAD_SIZE, (h + 1) * HEAD_SIZE)
        dq_ref[:, cols] = dqt[:, cols].T.astype(BF16)

    @pl.when((b == bc - 1) & (g < KVH - 1))
    def _():
        gather_event(g + 1, k)

    @pl.when((b == max(bc - 2, 0)) & (g < KVH - 2))
    def _():
        gather_event(g + 2, 0)

    @pl.when((b == bc - 1) & (g > 0))
    def _():
        reduce_event(g - 1, 3)

    @pl.when((b == bc - 1) & (g == KVH - 1))
    def _():
        for j in range(1, 4):
            reduce_event(g, j)
        for c in range(KVH):
            for s in range(k):
                exchange(c, s).wait_send()
            core_copy(c).wait_send()
            sent = r1.at[c]
            pltpu.make_async_copy(sent, sent, r1_sem.at[c, 0]).wait()
            sent = p2.at[c]
            pltpu.make_async_copy(sent, sent, r2_sem.at[c, 0]).wait()

        @pl.when(me < n - 1)
        def _():
            for c in range(KVH):
                window(c).wait_send()

        @pl.when(me > 0)
        def _():
            for c in range(KVH):
                back(c).wait_send()


def body(n, queries, keys, values, out_grad, links, header_blocks):
    rows = queries.shape[0]
    bc = rows // BLK
    nh = header_blocks.shape[0]
    cap = min(1 << log2(nh), n)
    tab_steps = log2(n) - log2(cap)
    span = (3 + nh) * BLK
    piece = 2 * nh * (BLK // n)
    wide = pl.BlockSpec((BLK, WIDE), lambda g, b: (b, g))
    whole = pl.BlockSpec((rows, KVH * HEAD_SIZE), lambda g, b: (0, 0))
    smem = pl.BlockSpec(memory_space=pltpu.SMEM)
    vmem = pltpu.VMEM
    dma = pltpu.SemaphoreType.DMA
    return pl.pallas_call(
        functools.partial(kernel, n, nh, bc),
        grid=(KVH, bc),
        in_specs=[smem, smem, wide, wide, whole, whole],
        out_specs=[wide, whole, whole],
        out_shape=[
            jax.ShapeDtypeStruct(queries.shape, BF16),
            jax.ShapeDtypeStruct(keys.shape, F32),
            jax.ShapeDtypeStruct(keys.shape, F32),
        ],
        scratch_shapes=[
            vmem((KVH, 2, WIN + rows, HEAD_SIZE), BF16),
            vmem((KVH, cap, 2, BLK, HEAD_SIZE), BF16),
            vmem((tab_steps + 1, KVH, 2, nh * BLK, HEAD_SIZE), BF16),
            vmem((tab_steps, KVH, 2, nh * BLK, HEAD_SIZE), BF16),
            vmem((span, HEAD_SIZE), BF16),
            vmem((span, HEAD_SIZE), BF16),
            vmem((span, WIDE), BF16),
            vmem((span, WIDE), BF16),
            vmem((KVH, 2, WIN + rows, HEAD_SIZE), F32),
            vmem((KVH, 2, WIN, HEAD_SIZE), BF16),
            vmem((KVH, 2, WIN, HEAD_SIZE), BF16),
            vmem((2, nh * BLK, HEAD_SIZE), F32),
            vmem((KVH, 2, n // 2, piece, HEAD_SIZE), BF16),
            vmem((KVH, n // 2, piece, HEAD_SIZE), BF16),
            vmem((KVH, n // 2, piece, HEAD_SIZE), BF16),
            vmem((KVH, n // 2 - 1, piece, HEAD_SIZE), BF16),
            vmem((KVH, nh, 2, BLK // n, HEAD_SIZE), F32),
            vmem((KVH, n - 1, 2, BLK // n, HEAD_SIZE), F32),
            vmem((KVH, n, 2, BLK // n, HEAD_SIZE), F32),
            dma((KVH, 2)),
            dma((KVH, log2(n))),
            dma((KVH, log2(n))),
            dma((KVH, 2)),
            dma((KVH, 2)),
            dma((KVH, 2)),
            dma((KVH, 2)),
        ],
        compiler_params=pltpu.CompilerParams(dimension_semantics=("arbitrary", "arbitrary"), collective_id=0,
                                             has_side_effects=True, vmem_limit_bytes=56 * 1024 * 1024),
        cost_estimate=pl.CostEstimate(flops=16_000_000_000, bytes_accessed=16_000_000, transcendentals=13_000_000),
        name="link_grads",
    )(links, header_blocks, queries, out_grad, keys, values)


def solution(mesh):
    row = P(("groups", "ctx"), None)
    return jax.shard_map(functools.partial(body, mesh.shape["ctx"]), mesh=mesh,
                         in_specs=(row, row, row, row, row, P("groups")), out_specs=(row, row, row), check_vma=False)
```

```python
import functools
import math

import jax
import jax.numpy as jnp
from jax import lax
from jax.experimental import pallas as pl
from jax.experimental.pallas import tpu as pltpu
from jax.sharding import PartitionSpec as P

QUERY_HEADS = 28
KVH = 4
HEAD_SIZE = 128
BLK = 128
WIN = 256
LINKS = 4
REP = QUERY_HEADS // KVH
WIDE = REP * HEAD_SIZE
SPAN = 3 * BLK
FACTOR = float(HEAD_SIZE) ** (-0.5)
EXP2_FACTOR = FACTOR * math.log2(math.e)
NT = (((1,), (1,)), ((), ()))
MESH = pl.DeviceIdType.MESH
F32 = jnp.float32
BF16 = jnp.bfloat16


def dot(a, b, dims=(((1,), (0,)), ((), ()))):
    return lax.dot_general(a, b, dims, preferred_element_type=F32)


def log2(n):
    return n.bit_length() - 1


def head(h):
    return slice(h * HEAD_SIZE, (h + 1) * HEAD_SIZE)


def remote(src, dst, send, recv, device):
    return pltpu.make_async_remote_copy(src_ref=src, dst_ref=dst, send_sem=send, recv_sem=recv,
                                        device_id={"ctx": device}, device_id_type=MESH)


def landed(ref, sem):
    pltpu.make_async_copy(ref, ref, sem).wait()


def kernel(n, nh, bc, links, headers, q_ref, o_ref, k_ref, v_ref, dq_ref, kg_ref, vg_ref,
           qv, ov, dqv, kvx, slot, raw, tab, rtab, table, kcat, vcat, ds_s, p_s, near, back_s, back_r, far,
           s0, r0, s1, r1, red, p2, r2, io_sem, win_sem, a_sem, d_sem, y_sem, g_sem, back_sem, rs_sem, r1_sem, r2_sem):
    me = lax.axis_index("ctx")
    core = lax.rem(me, 2)
    pair = me // 2
    rp = BLK // n
    rows = bc * BLK
    far_peers = n // 4
    holders = [headers[h] // bc for h in range(nh)]

    def peer(x):
        return jnp.bitwise_xor(me, x)

    def flag_of(x):
        return jnp.where(x, 1.0, 0.0).astype(F32)

    mine = []
    for i in range(bc):
        hit = headers[0] == me * bc + i
        for h in range(1, nh):
            hit = hit | (headers[h] == me * bc + i)
        mine.append(flag_of(hit))

    def load(c):
        cols = pl.ds(pl.multiple_of(c * WIDE, WIDE), WIDE)
        return (pltpu.make_async_copy(q_ref.at[:, cols], qv.at[c], io_sem.at[0, c]),
                pltpu.make_async_copy(o_ref.at[:, cols], ov.at[c], io_sem.at[1, c]))

    def save(c):
        cols = pl.ds(pl.multiple_of(c * WIDE, WIDE), WIDE)
        return pltpu.make_async_copy(dqv.at[c], dq_ref.at[:, cols], io_sem.at[2, c])

    def swap(c):
        return remote(slot.at[c, 1 - core], raw.at[c, 0, 1], a_sem.at[0, c], a_sem.at[1, c], peer(1))

    def spread(c, i):
        return remote(raw.at[c, 0], raw.at[c, i], d_sem.at[0, c], d_sem.at[1, c], peer(4 * i))

    def cross(c):
        return remote(tab.at[c], rtab.at[c], y_sem.at[0, c], y_sem.at[1, c], peer(2))

    def share(c):
        return remote(table.at[c, core], table.at[c, core], g_sem.at[0, c], g_sem.at[1, c], peer(1))

    def gather_event(c, j):
        if j == 0:
            swap(c).start()
        if j == 1:
            swap(c).wait_recv()
            raw[c, 0, 0] = slot[c, core]
            for i in range(1, far_peers):
                spread(c, i).start()
        if j == 2:
            landed(raw.at[c, pl.ds(1, far_peers - 1)], d_sem.at[1, c])
            for h in range(nh):
                total = jnp.zeros((BLK, HEAD_SIZE), F32)
                for i in range(far_peers):
                    for t in range(2):
                        total = total + raw[c, i, t].astype(F32) * flag_of(peer(holders[h]) == 4 * i + t)
                tab[c, h * BLK:(h + 1) * BLK] = total.astype(BF16)
            cross(c).start()
        if j == 3:
            cross(c).wait_recv()
            table[c, core] = (tab[c].astype(F32) + rtab[c].astype(F32)).astype(BF16)
            share(c).start()
        if j == 4:
            share(c).wait_recv()

    def window(c):
        return remote(kvx.at[c, :, pl.ds(rows, WIN)], kvx.at[c, :, pl.ds(0, WIN)], win_sem.at[0, c], win_sem.at[1, c],
                      lax.rem(me + 1, n))

    def back(c):
        return remote(back_s.at[c], back_r.at[c], back_sem.at[0, c], back_sem.at[1, c], lax.rem(me + n - 1, n))

    def core_copy(c):
        return remote(s0.at[c, 1 - core], r0.at[c], rs_sem.at[0, c], rs_sem.at[1, c], peer(1))

    def scatter_copy(c, i):
        return remote(s1.at[c, jnp.bitwise_xor(pair, i)], r1.at[c, i - 1], r1_sem.at[0, c], r1_sem.at[1, c], peer(2 * i))

    def return_copy(c, i):
        return remote(p2.at[c, i - 1], r2.at[c, me], r2_sem.at[0, c], r2_sem.at[1, c], peer(i))

    def rows_for(c, d):
        return sum(red[c, h] * flag_of(holders[h] == d) for h in range(nh))

    def reduce_event(c, j):
        if j == 0:
            for p in range(n):
                parts = [far[t, h * BLK + p * rp:h * BLK + (p + 1) * rp] for t in range(2) for h in range(nh)]
                s0[c, p % 2, p // 2] = jnp.concatenate(parts, axis=0).astype(BF16)
            core_copy(c).start()
        if j == 1:
            core_copy(c).wait_recv()
            s1[c] = (s0[c, core].astype(F32) + r0[c].astype(F32)).astype(BF16)
            for i in range(1, n // 2):
                scatter_copy(c, i).start()
        if j == 2:
            landed(r1.at[c], r1_sem.at[1, c])
            total = s1[c, pair].astype(F32)
            for i in range(n // 2 - 1):
                total = total + r1[c, i].astype(F32)
            for t in range(2):
                for h in range(nh):
                    at = (t * nh + h) * rp
                    red[c, h, t] = total[at:at + rp]
            for i in range(1, n):
                p2[c, i - 1] = rows_for(c, peer(i))
                return_copy(c, i).start()
            r2[c, me] = rows_for(c, me)
        if j == 3:
            landed(p2.at[c], r2_sem.at[1, c])
            cols = pl.ds(pl.multiple_of(c * HEAD_SIZE, HEAD_SIZE), HEAD_SIZE)
            for t, out in ((0, kg_ref), (1, vg_ref)):
                own = jnp.concatenate([r2[c, p, t] for p in range(n)], axis=0)
                for i in range(bc):
                    out[i * BLK:(i + 1) * BLK, cols] = near[c, t, WIN + i * BLK:WIN + (i + 1) * BLK] + own * mine[i]

            @pl.when(me < n - 1)
            def _():
                back(c).wait_recv()
                for t, out in ((0, kg_ref), (1, vg_ref)):
                    out[rows - WIN:rows, cols] = out[rows - WIN:rows, cols] + back_r[c, t].astype(F32)

    barrier = pltpu.get_barrier_semaphore()
    for i in range(1, n):
        pl.semaphore_signal(barrier, inc=1, device_id={"ctx": peer(i)}, device_id_type=MESH)
    for c in range(KVH):
        for copy in load(c):
            copy.start()
    for c in range(KVH):
        cols = head(c)
        for t, ref in enumerate((k_ref, v_ref)):
            slot[c, t] = sum(ref[i * BLK:(i + 1) * BLK, cols].astype(F32) * f for i, f in enumerate(mine)).astype(BF16)
            kvx[c, t, WIN:] = ref[:, cols]

    @pl.when(me == 0)
    def _():
        kvx[:, :, 0:WIN] = jnp.zeros((KVH, 2, WIN, HEAD_SIZE), BF16)

    pl.semaphore_wait(barrier, n - 1)
    for c in range(KVH):
        gather_event(c, 0)
    gather_event(0, 1)

    @pl.when(me < n - 1)
    def _():
        for c in range(KVH):
            window(c).start()

    gather_event(0, 2)
    gather_event(1, 1)
    gather_event(0, 3)
    gather_event(0, 4)

    pairs = [range(a, min(a + 2, REP)) for a in range(0, REP, 2)]

    def stacked(ref, g, b, heads):
        return jnp.concatenate([ref[g, b * BLK:(b + 1) * BLK, head(h)] for h in heads], axis=0)

    def prepare(g, b):
        at = b % 2
        kcat[at, 0:SPAN] = kvx[g, 0, b * BLK:b * BLK + SPAN]
        vcat[at, 0:SPAN] = kvx[g, 1, b * BLK:b * BLK + SPAN]
        kcat[at, SPAN:] = table[g, 0]
        vcat[at, SPAN:] = table[g, 1]

    def scores(g, b, heads):
        at = b % 2
        return (dot(kcat[at], stacked(qv, g, b, heads), NT), dot(vcat[at], stacked(ov, g, b, heads), NT))

    def soft(b, heads, st, dpt):
        at = b % 2
        first = me * bc + b
        dead0 = jnp.where(first >= 2, 0.0, 1e30).astype(F32)
        dead = [jnp.float32(0.0), jnp.where(first >= 1, 0.0, 1e30).astype(F32)]
        for h in range(nh):
            live = links[b, 0] == h
            for l in range(1, LINKS):
                live = live | (links[b, l] == h)
            dead.append(jnp.where(live, 0.0, 1e30).astype(F32))
        wide = len(heads) * BLK
        cols = slice(heads[0] * HEAD_SIZE, heads[0] * HEAD_SIZE + wide)
        key_at = lax.broadcasted_iota(jnp.int32, (BLK, wide), 0)
        query_at = lax.broadcasted_iota(jnp.int32, (BLK, wide), 1) & (BLK - 1)
        current = key_at <= query_at
        x = [jnp.where(current, st[2 * BLK:3 * BLK], st[0:BLK] - dead0)]
        d = [jnp.where(current, dpt[2 * BLK:3 * BLK], dpt[0:BLK])]
        for t in [1] + list(range(3, 3 + nh)):
            x.append(st[t * BLK:(t + 1) * BLK])
            d.append(dpt[t * BLK:(t + 1) * BLK])
        top = None
        for xt, dt in zip(x, dead):
            m = jnp.max(xt.reshape(BLK // 8, 8, wide), axis=0) - dt
            top = m if top is None else jnp.maximum(top, m)
        top = jnp.max(top, axis=0, keepdims=True)
        e = [jnp.exp2((xt - (top + dt)) * EXP2_FACTOR) for xt, dt in zip(x, dead)]
        norm = e[0]
        mixed = e[0] * d[0]
        for et, dt in zip(e[1:], d[1:]):
            norm = norm + et
            mixed = mixed + et * dt
        inverse = 1.0 / jnp.sum(norm, axis=0, keepdims=True)
        delta = jnp.sum(mixed, axis=0, keepdims=True) * inverse
        for t, (et, dt) in enumerate(zip(e, d)):
            p = et * inverse
            ds = p * (dt - delta)
            if t == 0:
                p_s[at, 2 * BLK:3 * BLK, cols] = jnp.where(current, p, 0.0).astype(BF16)
                p_s[at, 0:BLK, cols] = jnp.where(current, 0.0, p).astype(BF16)
                ds_s[at, 2 * BLK:3 * BLK, cols] = jnp.where(current, ds, 0.0).astype(BF16)
                ds_s[at, 0:BLK, cols] = jnp.where(current, 0.0, ds).astype(BF16)
            else:
                place = BLK if t == 1 else (t + 1) * BLK
                p_s[at, place:place + BLK, cols] = p.astype(BF16)
                ds_s[at, place:place + BLK, cols] = ds.astype(BF16)

    def key_part(g, b, lo, hi):
        at = b % 2
        for t, (w, ref) in enumerate(((ds_s, qv), (p_s, ov))):
            got = dot(w[at, lo:hi], stacked(ref, g, b, range(REP)))
            if t == 0:
                got = got * FACTOR
            mid = min(max(SPAN, lo), hi)
            if lo < mid:
                near[g, t, b * BLK + lo:b * BLK + mid] += got[0:mid - lo]
            if mid < hi:
                if b == 0:
                    far[t, mid - SPAN:hi - SPAN] = got[mid - lo:]
                else:
                    far[t, mid - SPAN:hi - SPAN] += got[mid - lo:]

    def query_part(g, b, heads):
        at = b % 2
        cols = slice(heads[0] * HEAD_SIZE, (heads[-1] + 1) * HEAD_SIZE)
        dqt = dot(kcat[at].T, ds_s[at, :, cols]) * FACTOR
        for i, h in enumerate(heads):
            dqv[g, b * BLK:(b + 1) * BLK, head(h)] = dqt[:, i * BLK:(i + 1) * BLK].T.astype(BF16)

    total = SPAN + nh * BLK
    parts = [(x, min(x + 2 * BLK, total)) for x in range(0, total, 2 * BLK)]
    parts = [parts[i::len(pairs)] for i in range(len(pairs))]

    def finish(g, b, i):
        for lo, hi in parts[i]:
            key_part(g, b, lo, hi)
        query_part(g, b, pairs[i])

    def events(g, b):
        if b == 0:
            @pl.when(g < KVH - 1)
            def _():
                gather_event(g + 1, 2)
        if b == min(1, bc - 1):
            @pl.when(g < KVH - 2)
            def _():
                gather_event(g + 2, 1)

            @pl.when(g > 0)
            def _():
                reduce_event(g - 1, 1)

            @pl.when(g > 1)
            def _():
                reduce_event(g - 2, 3)
        if b == min(2, bc - 1):
            @pl.when(g < KVH - 1)
            def _():
                gather_event(g + 1, 3)
        if b == bc - 1:
            @pl.when(g > 0)
            def _():
                reduce_event(g - 1, 2)

    def one(g, carry):
        for copy in load(g):
            copy.wait()

        @pl.when(me > 0)
        def _():
            window(g).wait_recv()

        near[g] = jnp.zeros(near.shape[1:], F32)
        for b in range(bc):
            events(g, b)
            prepare(g, b)
            got = scores(g, b, pairs[0])
            for i, heads in enumerate(pairs):
                later = scores(g, b, pairs[i + 1]) if i + 1 < len(pairs) else None
                soft(b, heads, *got)
                if b > 0:
                    finish(g, b - 1, i)
                got = later
        for i in range(len(pairs)):
            for lo, hi in parts[i]:
                key_part(g, bc - 1, lo, hi)
        reduce_event(g, 0)

        @pl.when(me > 0)
        def _():
            back_s[g] = near[g, :, 0:WIN].astype(BF16)
            back(g).start()

        for i in range(len(pairs)):
            query_part(g, bc - 1, pairs[i])
        save(g).start()

        @pl.when(g < KVH - 1)
        def _():
            gather_event(g + 1, 4)

        return carry

    lax.fori_loop(0, KVH, one, 0)

    reduce_event(KVH - 1, 1)
    reduce_event(KVH - 2, 3)
    reduce_event(KVH - 1, 2)
    for c in range(KVH):
        swap(c).wait_send()
        landed(raw.at[c, pl.ds(1, far_peers - 1)], d_sem.at[0, c])
        cross(c).wait_send()
        share(c).wait_send()
        core_copy(c).wait_send()
        landed(r1.at[c], r1_sem.at[0, c])
        landed(p2.at[c], r2_sem.at[0, c])
        save(c).wait()

    @pl.when(me < n - 1)
    def _():
        for c in range(KVH):
            window(c).wait_send()

    @pl.when(me > 0)
    def _():
        for c in range(KVH):
            back(c).wait_send()

    reduce_event(KVH - 1, 3)


def body(n, queries, keys, values, out_grad, links, header_blocks):
    rows = queries.shape[0]
    bc = rows // BLK
    nh = header_blocks.shape[0]
    span = SPAN + nh * BLK
    piece = 2 * nh * (BLK // n)
    smem = pl.BlockSpec(memory_space=pltpu.SMEM)
    whole = pl.BlockSpec(memory_space=pltpu.VMEM)
    hbm = pl.BlockSpec(memory_space=pl.ANY)
    vmem = pltpu.VMEM
    dma = pltpu.SemaphoreType.DMA
    return pl.pallas_call(
        functools.partial(kernel, n, nh, bc),
        in_specs=[smem, smem, hbm, hbm, whole, whole],
        out_specs=[hbm, whole, whole],
        out_shape=[
            jax.ShapeDtypeStruct(queries.shape, BF16),
            jax.ShapeDtypeStruct(keys.shape, F32),
            jax.ShapeDtypeStruct(keys.shape, F32),
        ],
        scratch_shapes=[
            vmem((KVH, rows, WIDE), BF16),
            vmem((KVH, rows, WIDE), BF16),
            vmem((KVH, rows, WIDE), BF16),
            vmem((KVH, 2, WIN + rows, HEAD_SIZE), BF16),
            vmem((KVH, 2, BLK, HEAD_SIZE), BF16),
            vmem((KVH, n // 4, 2, BLK, HEAD_SIZE), BF16),
            vmem((KVH, nh * BLK, HEAD_SIZE), BF16),
            vmem((KVH, nh * BLK, HEAD_SIZE), BF16),
            vmem((KVH, 2, nh * BLK, HEAD_SIZE), BF16),
            vmem((2, span, HEAD_SIZE), BF16),
            vmem((2, span, HEAD_SIZE), BF16),
            vmem((2, span, WIDE), BF16),
            vmem((2, span, WIDE), BF16),
            vmem((KVH, 2, WIN + rows, HEAD_SIZE), F32),
            vmem((KVH, 2, WIN, HEAD_SIZE), BF16),
            vmem((KVH, 2, WIN, HEAD_SIZE), BF16),
            vmem((2, nh * BLK, HEAD_SIZE), F32),
            vmem((KVH, 2, n // 2, piece, HEAD_SIZE), BF16),
            vmem((KVH, n // 2, piece, HEAD_SIZE), BF16),
            vmem((KVH, n // 2, piece, HEAD_SIZE), BF16),
            vmem((KVH, n // 2 - 1, piece, HEAD_SIZE), BF16),
            vmem((KVH, nh, 2, BLK // n, HEAD_SIZE), F32),
            vmem((KVH, n - 1, 2, BLK // n, HEAD_SIZE), F32),
            vmem((KVH, n, 2, BLK // n, HEAD_SIZE), F32),
            dma((3, KVH)),
        ] + [dma((2, KVH))] * 9,
        compiler_params=pltpu.CompilerParams(collective_id=0, has_side_effects=True,
                                             vmem_limit_bytes=58 * 1024 * 1024),
        cost_estimate=pl.CostEstimate(flops=16_000_000_000, bytes_accessed=16_000_000, transcendentals=13_000_000),
        name="link_grads",
    )(links, header_blocks, queries, out_grad, keys, values)


def solution(mesh):
    row = P(("groups", "ctx"), None)
    return jax.shard_map(functools.partial(body, mesh.shape["ctx"]), mesh=mesh,
                         in_specs=(row, row, row, row, row, P("groups")), out_specs=(row, row, row), check_vma=False)
```
